256 devices in a mesh: tm: 32 (over z, y), table: 8 (over x, core).
Axes of the slice: x: 4, y: 4, z: 8, core: 2. Of those that a mesh axis runs over, the one named last changes fastest.
Arguments:
- out_grad: bfloat16 [8, 65536, 512], P('table', 'tm'), may hold values from -1.1953125 to 1.1953125
- bc_proj: bfloat16 [8, 65536, 128], P('table', 'tm'), may hold values from -0.18847656 to 0.18847656
- decay_log: float32 [8, 8, 65536], P('table', None, 'tm'), may hold values from -1 to 0
- skip_gain: float32 [8], replicated, may hold values from 0.5 to 1.5
- owner: int32 [8, 65536, 1], P('table', 'tm'), may hold values from 0 to 255; in each aligned block of 2048 rows (0 to 2047, 2048 to 4095, ..., all dimensions but the last counted through in order) at most 16 rows name the same one
- item_row: int32 [8, 65536], P('table', 'tm'), may hold values from 0 to 1535
- table: bfloat16 [393216, 512], P(('tm', 'table')), may hold values from -3 to 3
- accum: float32 [393216, 512], P(('tm', 'table')), may hold values from 1 to 10
Outputs:
- new_table: bfloat16 [393216, 512], P(('tm', 'table'))
- new_accum: float32 [393216, 512], P(('tm', 'table'))
The draws below stay inside these ranges and needn't reach their ends.
Inputs may be any that keep to these rules, and one draw needn't show every extreme that they name: Among the events of one device at most 16 have the same owner; in every draw some device has exactly 16 events for some owner.
All inputs are finite; a program needn't handle non-finite values.
Results may differ from the reference program's by a relative error of at most 0.0018.
Values may be sent and summed in bfloat16 or wider, within the bound.
A program may use at most 128 MiB of HBM per device.

```python
import math
import jax
import jax.numpy as jnp
import numpy as np
from jax import lax

D = 512
HEADS = 8
HEAD_DIM = 64
STATE = 64
GROUP = 256
EV_DEV = 2048
USR_DEV = 1
V_OWN = 1536
EVENT_LENGTH = 65536
USER_COUNT = 8
ITEMS = 393216
CAP = 16
DEVICES = 256


def draw_decay_log(key, part):
    random_keys = jax.random.split(key, 7)
    fast_share = 0.5
    fast = jax.random.bernoulli(random_keys[0], fast_share, (USER_COUNT, HEADS, 1)).astype(jnp.float32)
    fast_rate = jnp.exp(jax.random.uniform(random_keys[1], (USER_COUNT, HEADS, 1), jnp.float32, math.log(1.0 / 50.0), math.log(1.0 / 30.0)))
    slow_rate = 0.5 / EVENT_LENGTH * jax.random.uniform(random_keys[2], (USER_COUNT, HEADS, 1), jnp.float32, 0.5, 1.0)
    baseline_value = fast * fast_rate + (1.0 - fast) * slow_rate
    approximate_value = jnp.exp(jax.random.uniform(random_keys[3], (USER_COUNT, HEADS, EVENT_LENGTH), jnp.float32, -0.7, 0.7))
    approximate_grid = jnp.exp(jax.random.uniform(random_keys[4], (USER_COUNT, HEADS, EVENT_LENGTH // GROUP), jnp.float32, -0.7, 0.7))
    approximate_grid = jnp.repeat(approximate_grid, GROUP, axis=2)
    spike_position = jax.random.bernoulli(random_keys[5], 4.0 / EVENT_LENGTH, (USER_COUNT, 1, EVENT_LENGTH)).astype(jnp.float32)
    spike_events = spike_position * jnp.log(jax.random.uniform(random_keys[6], (USER_COUNT, 1, EVENT_LENGTH), jnp.float32, 0.5, 0.8))
    return -baseline_value * approximate_value * approximate_grid + spike_events


def place_ends(array, key, least, top_value):
    longest = array.shape.index(max(array.shape))
    spots = []
    for shift in (0, 1):
        where = [jax.random.randint(jax.random.fold_in(key, axis), (), 0, length) for axis, length in enumerate(array.shape)]
        where[longest] = (where[longest] + shift) % array.shape[longest]
        spots.append(tuple(where))
    return array.at[spots[0]].set(least).at[spots[1]].set(top_value)


def steps_of(stream_key, shape, pieces, least, largest):
    level, own = 1.0, jax.random.fold_in(stream_key, 6)
    for dim, blocks in pieces:
        heights = jnp.exp(jax.random.uniform(jax.random.fold_in(own, dim), (blocks,), jnp.float32, least / len(pieces), largest / len(pieces)))
        level = level * jnp.repeat(heights, shape[dim] // blocks).reshape([-1 if axis == dim else 1 for axis in range(len(shape))])
    return level


def routed_block(own_key, own, number, rows, count, top, bound, slope):
    sequence = jax.random.permutation(own_key, count)
    crowded, ordinary = portions_of(count, rows * top, bound, slope, True), portions_of(count, rows * top, bound, slope, False)
    places = jnp.arange(count)

    def named(lengths, rotation):
        used = int((lengths > 0).sum())
        fixed = max(1, used // 4)
        shifted = fixed + (places - fixed + rotation * (used - fixed)) % max(1, count - fixed)
        return jnp.zeros((count,), jnp.int32).at[sequence[jnp.where(places < fixed, places, shifted)]].set(jnp.asarray(lengths, jnp.int32))

    lengths = jnp.where(number % 4 == 0, named(crowded, number // 4), named(ordinary, number - number // 4 - 1))
    mixed = jax.random.permutation(jax.random.fold_in(own, 3), count)
    source_of, sink = mixed[0:count // 2 * 2:2], mixed[1:count // 2 * 2:2]
    room = jnp.minimum(lengths[source_of] - 1, bound - lengths[sink]) // 2
    room = jnp.where((source_of == sequence[0]) | (sink == sequence[0]) | (lengths[sink] == 0), 0, jnp.maximum(room, 0))
    shifted = jax.random.randint(jax.random.fold_in(own, 4), (count // 2,), 0, 1 << 20) % (room + 1)
    lengths = lengths.at[source_of].add(-shifted).at[sink].add(shifted)
    members = jnp.searchsorted(jnp.cumsum(lengths), jnp.arange(rows * top), side="right").astype(jnp.int32)
    grid = members.reshape(top, rows).T
    grid = grid[jax.random.permutation(jax.random.fold_in(own, 1), rows)]
    rotation = jax.random.randint(jax.random.fold_in(own, 2), (rows, 1), 0, top)
    return jnp.take_along_axis(grid, (jnp.arange(top)[None, :] + rotation) % top, axis=1)


def portions_of(count, total, most, slope, full):
    weights = [(1 << 20) // math.isqrt(standing ** slope) + 1 for standing in range(1, count + 1)]
    largest = most if full else min(most, max(-(-total // count), total * weights[0] // sum(weights)))
    least = 1 if total - largest >= count - 1 else 0
    given, spare = [largest] + [least] * (count - 1), total - largest - least * (count - 1)
    while spare > 0:
        movable = [i for i in range(1, count) if given[i] < largest] or [i for i in range(1, count) if given[i] < most]
        whole, left = sum([weights[i] for i in movable]), spare
        for i in movable:
            extra = min(most - given[i], max(1, left * weights[i] // whole), spare)
            given[i] = given[i] + extra
            spare = spare - extra
    return np.array(given)


def centred(own_key, dims, width, reach, cuts=(), held_as=jnp.bfloat16):
    entries = width * jax.random.normal(own_key, dims, jnp.float32)
    if cuts:
        entries = entries * steps_of(own_key, dims, cuts, -0.22, 0.18)
    return jnp.clip(entries, -reach, reach).astype(held_as)


def setup_inputs(seed: int = 0) -> dict:
    keys = jax.random.split(jax.random.key(seed), 9)
    out_grad = centred(keys[0], (USER_COUNT, EVENT_LENGTH, D), 0.2, 1.1953125, ((0, 8), (1, 32)))
    bc_proj = centred(keys[1], (USER_COUNT, EVENT_LENGTH, 2 * STATE), (0.6 / (EV_DEV * STATE) ** 0.25), 0.18847656, ((0, 8), (1, 32)))
    decay_log = draw_decay_log(jax.random.fold_in(keys[8], 71), 0)
    skip_gain = jnp.clip(jax.random.uniform(keys[3], (HEADS,), jnp.float32, 0.5, 1.5), 0.5, 1.5)
    owner_keys = jax.random.split(jax.random.fold_in(keys[4], 1), USER_COUNT * EVENT_LENGTH // (USR_DEV * EV_DEV))
    owner_turns = jax.random.permutation(jax.random.fold_in(keys[4], 3), USER_COUNT * EVENT_LENGTH // (USR_DEV * EV_DEV))
    owner = jax.vmap(lambda own, number: routed_block(jax.random.fold_in(keys[4], 2), own, number, USR_DEV * EV_DEV, DEVICES, 1, CAP, 2))(owner_keys, owner_turns).reshape((USER_COUNT, EVENT_LENGTH, 1))
    item_row = place_ends(jax.random.randint(keys[5], (USER_COUNT, EVENT_LENGTH), 0, V_OWN), jax.random.fold_in(keys[5], 1), 0, V_OWN - 1).astype(jnp.int32)
    table = centred(keys[6], (ITEMS, D), 0.5, 3.0, ((0, 256),))
    accum = jnp.clip(jnp.exp(math.log(10.0) - 2.3025851 * jax.random.uniform(keys[7], (ITEMS, D), jnp.float32) ** steps_of(keys[7], (ITEMS, D), ((0, 256),), -0.2, 0.2)), 1.0, 10.0)
    return dict(out_grad=out_grad, bc_proj=bc_proj, decay_log=decay_log, skip_gain=skip_gain, owner=owner, item_row=item_row, table=table, accum=accum)


learn_rate = 1.0

def block_end(grad_block, c_block, decay_block):
    cumul = jnp.cumsum(decay_block, axis=1)
    length = grad_block.shape[0]
    scaled = grad_block.astype(jnp.float32).reshape(length, HEADS, -1) * jnp.exp(cumul).T[:, :, None]
    ends = jnp.einsum('thp,tn->hpn', scaled, c_block.astype(jnp.float32), precision=lax.Precision.HIGHEST)
    return (cumul[:, -1], ends)

def fold_back(carry, item):
    log_end, end_term = item
    return (end_term + jnp.exp(log_end)[:, None, None] * carry, carry)

def block_rows(grad_block, b_block, c_block, decay_block, carried, skip_gain):
    length = grad_block.shape[0]
    cumul = jnp.cumsum(decay_block, axis=1)
    scores = jnp.dot(c_block, b_block.T, preferred_element_type=jnp.float32)
    later = jnp.arange(length)[:, None] >= jnp.arange(length)[None, :]
    gaps = jnp.where(later[None], cumul[:, :, None] - cumul[:, None, :], 0.0)
    mixing = jnp.where(later[None], jnp.exp(gaps) * scores[None], 0.0).astype(jnp.bfloat16)
    heads_grad = grad_block.reshape(length, HEADS, -1)
    inner = jnp.einsum('hts,thp->shp', mixing.astype(jnp.float32), heads_grad.astype(jnp.float32))
    fading = jnp.exp(cumul[:, -1:] - cumul)
    carried_part = jnp.einsum('hpn,sn->shp', carried, b_block.astype(jnp.float32), precision=lax.Precision.HIGHEST) * fading.T[:, :, None]
    total = inner + carried_part + skip_gain[None, :, None] * heads_grad.astype(jnp.float32)
    return total.reshape(length, -1).astype(jnp.bfloat16)

def reference(out_grad, bc_proj, decay_log, skip_gain, owner, item_row, table, accum):
    blocks = EVENT_LENGTH // GROUP
    item = (owner[:, :, 0] * V_OWN + item_row).astype(jnp.int32)

    def user_step(total, inputs):
        grad_user, bc_user, decay_user, item_user = inputs
        grad_blocks = grad_user.reshape(blocks, GROUP, D)
        b_blocks = bc_user[:, :STATE].reshape(blocks, GROUP, STATE)
        c_blocks = bc_user[:, STATE:].reshape(blocks, GROUP, STATE)
        decay_blocks = decay_user.reshape(HEADS, blocks, GROUP).transpose(1, 0, 2)
        log_ends, end_terms = lax.map(lambda a: block_end(a[0], a[1], a[2]), (grad_blocks, c_blocks, decay_blocks))
        start = jnp.zeros((HEADS, HEAD_DIM, STATE), jnp.float32)
        _, carried = lax.scan(fold_back, start, (log_ends, end_terms), reverse=True)
        rows = lax.map(lambda a: block_rows(a[0], a[1], a[2], a[3], a[4], skip_gain), (grad_blocks, b_blocks, c_blocks, decay_blocks, carried))
        total = total.at[item_user].add(rows.reshape(EVENT_LENGTH, D).astype(jnp.float32))
        return (total, 0)
    zeros = jnp.zeros((ITEMS, D), jnp.float32)
    item_grad, _ = lax.scan(user_step, zeros, (out_grad, bc_proj, decay_log, item))
    new_accum = accum + item_grad * item_grad
    new_table = (table.astype(jnp.float32) - learn_rate * item_grad / jnp.sqrt(new_accum)).astype(jnp.bfloat16)
    return (new_table, new_accum)
```

```python
import functools

import jax
import jax.numpy as jnp
from jax import lax
from jax.experimental import pallas as pl
from jax.experimental.pallas import tpu as pltpu
from jax.sharding import PartitionSpec as P

HEADS = 8
STATE = 64
GROUP = 256
CAP = 16
LANES = 128
RATE = 1.0
F32 = jnp.float32
BF16 = jnp.bfloat16


def dims(lhs, rhs):
    return (((lhs,), (rhs,)), ((), ()))


def spread(column, width):
    heads = lax.broadcasted_iota(jnp.int32, (HEADS, width), 0)
    owner = lax.broadcasted_iota(jnp.int32, (HEADS, width), 1) // (width // HEADS)
    pick = (heads == owner).astype(BF16)
    high = column.astype(BF16)
    low = (column - high.astype(F32)).astype(BF16)
    return jnp.dot(high, pick, preferred_element_type=F32) + jnp.dot(
        low, pick, preferred_element_type=F32
    )


def column_sums(decay):
    at = lax.broadcasted_iota(jnp.int32, (GROUP, GROUP), 0)
    before = lax.broadcasted_iota(jnp.int32, (GROUP, GROUP), 1)
    upto = (before <= at).astype(F32)
    return lax.dot_general(
        upto, decay, dims(1, 1), precision=lax.Precision.HIGHEST, preferred_element_type=F32
    )


def row_sums(decay):
    before = lax.broadcasted_iota(jnp.int32, (GROUP, GROUP), 0)
    at = lax.broadcasted_iota(jnp.int32, (GROUP, GROUP), 1)
    upto = (before <= at).astype(F32)
    return jnp.dot(decay, upto, precision=lax.Precision.HIGHEST, preferred_element_type=F32)


def route_kernel(owner_ref, row_ref, place_ref, ids_ref):
    holders = ids_ref.shape[0]
    blocks = owner_ref.shape[0]
    holder = lax.broadcasted_iota(jnp.int32, (holders, GROUP), 0)
    earlier = (
        lax.broadcasted_iota(jnp.int32, (GROUP, GROUP), 0)
        < lax.broadcasted_iota(jnp.int32, (GROUP, GROUP), 1)
    ).astype(BF16)
    slots = lax.broadcasted_iota(jnp.int32, (CAP, GROUP), 0)
    carry = jnp.zeros((holders, 1), F32)
    ids = jnp.zeros((holders, 2 * CAP), F32)
    for b in range(blocks):
        own = owner_ref[b : b + 1, :]
        hit = holder == own
        hits = jnp.where(hit, 1.0, 0.0).astype(F32)
        hits_low = hits.astype(BF16)
        before = jnp.dot(hits_low, earlier, preferred_element_type=F32) + carry
        slot = jnp.sum(hits * before, axis=0, keepdims=True).astype(jnp.int32)
        carry = carry + jnp.sum(hits, axis=1, keepdims=True)
        place_ref[b : b + 1, :] = own * CAP + slot
        mark = row_ref[b : b + 1, :] + 1
        high = lax.shift_right_logical(mark, 6)
        low = lax.bitwise_and(mark, 63)
        chosen = slots == slot
        table = jnp.concatenate(
            [
                jnp.where(chosen, high, 0).astype(F32),
                jnp.where(chosen, low, 0).astype(F32),
            ],
            axis=0,
        ).astype(BF16)
        ids = ids + lax.dot_general(hits_low, table, dims(1, 1), preferred_element_type=F32)
    total = ids[:, :CAP] * 64.0 + ids[:, CAP:] - 1.0
    ids_ref[...] = total.astype(jnp.int32)


def ends_kernel(grad_ref, bc_ref, decay_ref, ends_ref, fall_ref, send_ref, state, decayed):
    step = pl.program_id(0)
    width = grad_ref.shape[1]

    @pl.when(step == 0)
    def _():
        state[...] = jnp.zeros_like(state)
        decayed[...] = jnp.ones_like(decayed)

    factor = spread(jnp.exp(column_sums(decay_ref[...])), width)
    scaled = grad_ref[...].astype(F32) * factor
    high = scaled.astype(BF16)
    low = (scaled - high.astype(F32)).astype(BF16)
    c_turned = bc_ref[...].astype(F32).T[STATE:, :].astype(BF16)
    ends = jnp.dot(c_turned, high, preferred_element_type=F32) + jnp.dot(
        c_turned, low, preferred_element_type=F32
    )
    fall = factor[GROUP - 1 : GROUP, :]
    ends_ref[...] = ends
    fall_ref[...] = jnp.broadcast_to(fall, fall_ref.shape)
    state[...] = ends + fall * state[...]
    decayed[...] = decayed[...] * fall

    @pl.when(step == pl.num_programs(0) - 1)
    def _():
        tiles = width // LANES
        for r in range(STATE // 8):
            for j in range(tiles):
                lanes = slice(j * LANES, (j + 1) * LANES)
                send_ref[r * tiles + j, 0] = state[8 * r : 8 * r + 8, lanes]
                send_ref[r * tiles + j, 1] = decayed[:, lanes]


def within_kernel(grad_ref, bc_ref, decay_ref, skip_ref, out_ref):
    width = grad_ref.shape[1]
    head_dim = width // HEADS
    rows = row_sums(decay_ref[...])
    columns = column_sums(decay_ref[...])
    b_part = bc_ref[:, :STATE]
    c_part = bc_ref[:, STATE:]
    scores = lax.dot_general(b_part, c_part, dims(1, 1), preferred_element_type=F32)
    lane = lax.broadcasted_iota(jnp.int32, (GROUP, LANES), 1)
    source = lax.broadcasted_iota(jnp.int32, (GROUP, GROUP), 0)
    later = lax.broadcasted_iota(jnp.int32, (GROUP, GROUP), 1)
    keep = later >= source
    per_tile = LANES // head_dim
    for j in range(width // LANES):
        lanes = slice(j * LANES, (j + 1) * LANES)
        grad = grad_ref[:, lanes]
        total = None
        for i in range(per_tile):
            h = j * per_tile + i
            gaps = rows[h : h + 1, :] - columns[:, h : h + 1]
            mixing = (jnp.exp(jnp.where(keep, gaps, -1e30)) * scores).astype(BF16)
            part = jnp.dot(mixing, grad, preferred_element_type=F32)
            part = part + skip_ref[h] * grad.astype(F32)
            total = part if total is None else jnp.where(lane >= i * head_dim, part, total)
        out_ref[:, lanes] = total


def scan_kernel(got_ref, out_ref):
    count = got_ref.shape[0]
    held = jnp.zeros(out_ref.shape[1:], F32)
    for at in range(count - 1, -1, -1):
        out_ref[at] = held
        held = got_ref[at, 0] + got_ref[at, 1] * held


def rows_kernel(
    place_ref, part_ref, bc_ref, decay_ref, ends_ref, fall_ref, in_ref, out_ref, carried, flat, packed
):
    step = pl.program_id(0)
    last = pl.num_programs(0) - 1
    width = part_ref.shape[1]
    tiles = width // LANES

    @pl.when(step == 0)
    def _():
        packed[...] = jnp.zeros_like(packed)
        for r in range(STATE // 8):
            for j in range(tiles):
                carried[8 * r : 8 * r + 8, j * LANES : (j + 1) * LANES] = in_ref[r * tiles + j]

    sums = column_sums(decay_ref[...])
    fading = spread(jnp.exp(sums[GROUP - 1 : GROUP, :] - sums), width)
    held = carried[...]
    high = held.astype(BF16)
    low = (held - high.astype(F32)).astype(BF16)
    b_part = bc_ref[:, :STATE]
    product = jnp.dot(b_part, high, preferred_element_type=F32) + jnp.dot(
        b_part, low, preferred_element_type=F32
    )
    rows = (part_ref[...] + product * fading).astype(BF16).astype(F32)
    carried[...] = ends_ref[...] + fall_ref[0:1, :] * held
    for j in range(tiles):
        flat[pl.ds(j, GROUP, stride=tiles), :] = rows[:, j * LANES : (j + 1) * LANES]
    block = last - step

    def place(s, carry):
        for i in range(8):
            at = s * 8 + i
            to = place_ref[block, at]
            packed[pl.ds(pl.multiple_of(to * tiles, tiles), tiles), :] = flat[
                pl.ds(pl.multiple_of(at * tiles, tiles), tiles), :
            ]
        return carry

    lax.fori_loop(0, GROUP // 8, place, 0)

    @pl.when(step == last)
    def _():
        chunk = 256

        def put(c, carry):
            for j in range(tiles):
                start = c * chunk * tiles + j
                out_ref[pl.ds(pl.multiple_of(c * chunk, chunk), chunk), j * LANES : (j + 1) * LANES] = packed[
                    pl.ds(start, chunk, stride=tiles), :
                ].astype(BF16)
            return carry

        lax.fori_loop(0, out_ref.shape[0] // chunk, put, 0)


def update_kernel(ids_ref, rows_ref, table_ref, accum_ref, new_table_ref, new_accum_ref):
    tall = table_ref.shape[0]
    base = pl.program_id(0) * tall
    own = lax.broadcasted_iota(jnp.int32, (tall, ids_ref.shape[1]), 0) + base
    hits = jnp.where(own == ids_ref[...], 1.0, 0.0).astype(BF16)
    summed = jnp.dot(hits, rows_ref[...], preferred_element_type=F32)
    accum = accum_ref[...] + summed * summed
    new_accum_ref[...] = accum
    new_table_ref[...] = (
        table_ref[...].astype(F32) - RATE * summed / jnp.sqrt(accum)
    ).astype(BF16)


def on_device(out_grad, bc_proj, decay_log, skip_gain, owner, item_row, table, accum):
    users, events, width = out_grad.shape
    blocks = events // GROUP
    tm_count = lax.axis_size("tm")
    holders = tm_count * lax.axis_size("table")
    grad = out_grad.reshape(events, width)
    bc = bc_proj.reshape(events, 2 * STATE)
    decay = decay_log.reshape(HEADS, events)
    vmem = pl.BlockSpec(memory_space=pltpu.VMEM)
    smem = pl.BlockSpec(memory_space=pltpu.SMEM)

    places, ids = pl.pallas_call(
        route_kernel,
        name="route",
        out_shape=(
            jax.ShapeDtypeStruct((blocks, GROUP), jnp.int32),
            jax.ShapeDtypeStruct((holders, CAP), jnp.int32),
        ),
        in_specs=[vmem, vmem],
        out_specs=(vmem, vmem),
    )(owner.reshape(blocks, GROUP), item_row.reshape(blocks, GROUP))
    got_ids = lax.all_to_all(ids, ("tm", "table"), split_axis=0, concat_axis=0, tiled=True)

    def back(n, second=0):
        return lambda i: (blocks - 1 - i, 0)

    grad_spec = pl.BlockSpec((GROUP, width), lambda i: (blocks - 1 - i, 0))
    bc_spec = pl.BlockSpec((GROUP, 2 * STATE), lambda i: (blocks - 1 - i, 0))
    decay_spec = pl.BlockSpec((HEADS, GROUP), lambda i: (0, blocks - 1 - i))
    ends_spec = pl.BlockSpec((STATE, width), lambda i: (blocks - 1 - i, 0))
    fall_spec = pl.BlockSpec((8, width), lambda i: (blocks - 1 - i, 0))
    ends, falls, state = pl.pallas_call(
        ends_kernel,
        name="ends",
        grid=(blocks,),
        out_shape=(
            jax.ShapeDtypeStruct((blocks * STATE, width), F32),
            jax.ShapeDtypeStruct((blocks * 8, width), F32),
            jax.ShapeDtypeStruct((tm_count, 2, 8, LANES), F32),
        ),
        in_specs=[grad_spec, bc_spec, decay_spec],
        out_specs=(
            ends_spec,
            fall_spec,
            pl.BlockSpec((tm_count, 2, 8, LANES), lambda i: (0, 0, 0, 0)),
        ),
        scratch_shapes=[pltpu.VMEM((STATE, width), F32), pltpu.VMEM((8, width), F32)],
    )(grad, bc, decay)
    got_state = lax.all_to_all(state, "tm", split_axis=0, concat_axis=0, tiled=True)

    part = pl.pallas_call(
        within_kernel,
        name="within",
        grid=(blocks,),
        out_shape=jax.ShapeDtypeStruct((events, width), F32),
        in_specs=[grad_spec, bc_spec, decay_spec, smem],
        out_specs=grad_spec,
        cost_estimate=pl.CostEstimate(
            flops=2 * events * GROUP * (width * 2 + STATE),
            bytes_accessed=events * width * 6,
            transcendentals=events * GROUP * HEADS,
        ),
    )(grad, bc, decay, skip_gain)

    entering = pl.pallas_call(
        scan_kernel,
        name="scan",
        out_shape=jax.ShapeDtypeStruct((tm_count, 8, LANES), F32),
        in_specs=[vmem],
        out_specs=vmem,
    )(got_state)
    incoming = lax.all_to_all(entering, "tm", split_axis=0, concat_axis=0, tiled=True)

    slots = holders * CAP
    tiles = width // LANES
    send = pl.pallas_call(
        rows_kernel,
        name="rows",
        grid=(blocks,),
        out_shape=jax.ShapeDtypeStruct((slots, width), BF16),
        in_specs=[
            smem,
            grad_spec,
            bc_spec,
            decay_spec,
            ends_spec,
            fall_spec,
            pl.BlockSpec((tm_count, 8, LANES), lambda i: (0, 0, 0)),
        ],
        out_specs=pl.BlockSpec((slots, width), lambda i: (0, 0)),
        scratch_shapes=[
            pltpu.VMEM((STATE, width), F32),
            pltpu.VMEM((GROUP * tiles, LANES), F32),
            pltpu.VMEM((slots * tiles, LANES), F32),
        ],
    )(places, part, bc, decay, ends, falls, incoming)

    got = lax.all_to_all(
        send.reshape(holders, CAP, width), ("tm", "table"), split_axis=0, concat_axis=0, tiled=True
    )

    owned = table.shape[0]
    tall = 256
    tile = pl.BlockSpec((tall, width), lambda i: (i, 0))
    return pl.pallas_call(
        update_kernel,
        name="update",
        grid=(owned // tall,),
        out_shape=(
            jax.ShapeDtypeStruct((owned, width), BF16),
            jax.ShapeDtypeStruct((owned, width), F32),
        ),
        in_specs=[
            pl.BlockSpec((1, slots), lambda i: (0, 0)),
            pl.BlockSpec((slots, width), lambda i: (0, 0)),
            tile,
            tile,
        ],
        out_specs=(tile, tile),
    )(got_ids.reshape(1, slots), got.reshape(slots, width), table, accum)


def solution(mesh):
    placed = (
        P("table", "tm", None),
        P("table", "tm", None),
        P("table", None, "tm"),
        P(),
        P("table", "tm", None),
        P("table", "tm"),
        P(("tm", "table"), None),
        P(("tm", "table"), None),
    )
    return jax.shard_map(
        on_device,
        mesh=mesh,
        in_specs=placed,
        out_specs=(P(("tm", "table"), None), P(("tm", "table"), None)),
        check_vma=False,
    )
```

```python
import functools

import jax
import jax.numpy as jnp
from jax import lax
from jax.experimental import pallas as pl
from jax.experimental.pallas import tpu as pltpu
from jax.sharding import PartitionSpec as P

HEADS = 8
STATE = 64
GROUP = 256
CAP = 16
LANES = 128
RATE = 1.0
F32 = jnp.float32
BF16 = jnp.bfloat16


def dims(lhs, rhs):
    return (((lhs,), (rhs,)), ((), ()))


MESH = pl.DeviceIdType.MESH


def spread(column, width):
    heads = lax.rem(lax.broadcasted_iota(jnp.int32, (2 * HEADS, width), 0), HEADS)
    owner = lax.broadcasted_iota(jnp.int32, (2 * HEADS, width), 1) // (width // HEADS)
    pick = jnp.where(heads == owner, 1.0, 0.0).astype(BF16)
    high = column.astype(BF16).astype(F32)
    both = jnp.concatenate([high, column - high], axis=1).astype(BF16)
    return jnp.dot(both, pick, preferred_element_type=F32)


def split(value, axis):
    high = value.astype(BF16)
    low = (value - high.astype(F32)).astype(BF16)
    return jnp.concatenate([high, low], axis=axis)


def route(owner_ref, row_ref, place_ref, holders):
    blocks = owner_ref.shape[1] // GROUP
    holder = lax.broadcasted_iota(jnp.int32, (holders, GROUP), 0)
    earlier = jnp.where(
        lax.broadcasted_iota(jnp.int32, (GROUP, GROUP), 0)
        < lax.broadcasted_iota(jnp.int32, (GROUP, GROUP), 1),
        1.0,
        0.0,
    ).astype(BF16)
    slots = lax.broadcasted_iota(jnp.int32, (LANES, GROUP), 0)
    carry = jnp.zeros((holders, 1), F32)
    ids = jnp.zeros((holders, LANES), F32)
    for b in range(blocks):
        part = slice(b * GROUP, (b + 1) * GROUP)
        own = owner_ref[:, part]
        hits = jnp.where(holder == own, 1.0, 0.0)
        hits_low = hits.astype(BF16)
        before = jnp.dot(hits_low, earlier, preferred_element_type=F32) + carry
        slot = jnp.sum(hits * before, axis=0, keepdims=True).astype(jnp.int32)
        carry = carry + jnp.sum(hits, axis=1, keepdims=True)
        place_ref[b : b + 1, :] = own * CAP + slot
        mark = row_ref[:, part] + 1
        chosen = slots == slot
        high = jnp.where(chosen, lax.shift_right_logical(mark, 6).astype(F32), 0.0).astype(BF16)
        low = jnp.where(chosen, lax.bitwise_and(mark, 63).astype(F32), 0.0).astype(BF16)
        ids = ids + 64.0 * lax.dot_general(
            hits_low, high, dims(1, 1), preferred_element_type=F32
        )
        ids = ids + lax.dot_general(hits_low, low, dims(1, 1), preferred_element_type=F32)
    return ids - 1.0


def front_kernel(
    tm_count,
    table_count,
    owner_ref,
    row_ref,
    grad_ref,
    bc_ref,
    decay_ref,
    skip_ref,
    flat_ref,
    place_ref,
    ids_ref,
    columns,
    sums,
    ends,
    falls,
    part,
    state,
    decayed,
    send,
    got,
    entering,
    incoming,
    ids_send,
    ids_got,
    send_sems,
    recv_sems,
    back_send_sems,
    back_recv_sems,
    ids_send_sems,
    ids_recv_sems,
):
    tm, tb = lax.axis_index("tm"), lax.axis_index("table")
    events, width = grad_ref.shape
    blocks = events // GROUP
    head_dim = width // HEADS
    tiles = width // LANES
    per_tile = LANES // head_dim

    barrier = pltpu.get_barrier_semaphore()

    def greet_tm(d, carry):
        pl.semaphore_signal(
            barrier, inc=1, device_id=(lax.rem(tm + d, tm_count), tb), device_id_type=MESH
        )
        return carry

    def greet_table(d, carry):
        pl.semaphore_signal(
            barrier, inc=1, device_id=(tm, lax.rem(tb + d, table_count)), device_id_type=MESH
        )
        return carry

    lax.fori_loop(1, tm_count, greet_tm, 0)
    lax.fori_loop(1, table_count, greet_table, 0)

    upto = jnp.where(
        lax.broadcasted_iota(jnp.int32, (GROUP, GROUP), 0)
        <= lax.broadcasted_iota(jnp.int32, (GROUP, GROUP), 1),
        1.0,
        0.0,
    )
    decays = jnp.concatenate(
        [decay_ref[:, b * GROUP : (b + 1) * GROUP] for b in range(blocks)], axis=0
    )
    running = jnp.dot(decays, upto, precision=lax.Precision.HIGHEST, preferred_element_type=F32)
    sums[...] = running
    for b in range(blocks):
        columns[b * GROUP : (b + 1) * GROUP, :] = running[b * HEADS : (b + 1) * HEADS, :].T

    state[...] = jnp.zeros_like(state)
    decayed[...] = jnp.ones_like(decayed)

    def block_at(b, tall):
        return pl.ds(pl.multiple_of(b * tall, tall), tall)

    def end(i, carry):
        b = blocks - 1 - i
        here = block_at(b, GROUP)
        factor = spread(jnp.exp(columns[here, :]), width)
        scaled = grad_ref[here, :].astype(F32) * factor
        high = scaled.astype(BF16)
        low = (scaled - high.astype(F32)).astype(BF16)
        c_turned = bc_ref[here, :].astype(F32).T[STATE:, :].astype(BF16)
        term = jnp.dot(c_turned, high, preferred_element_type=F32) + jnp.dot(
            c_turned, low, preferred_element_type=F32
        )
        fall = factor[GROUP - 1 : GROUP, :]
        ends[block_at(b, STATE), :] = term
        falls[block_at(b, 8), :] = jnp.broadcast_to(fall, (8, width))
        state[...] = term + fall * state[...]
        decayed[...] = decayed[...] * fall
        return carry

    lax.fori_loop(0, blocks, end, 0)
    for r in range(STATE // 8):
        for j in range(tiles):
            lanes = slice(j * LANES, (j + 1) * LANES)
            send[r * tiles + j, 0] = state[8 * r : 8 * r + 8, lanes]
            send[r * tiles + j, 1] = decayed[:, lanes]
    ids = route(owner_ref, row_ref, place_ref, tm_count * table_count)
    send[:, 2] = ids.reshape(tm_count, table_count, LANES)

    pl.semaphore_wait(barrier, tm_count + table_count - 2)

    def outward(d):
        to = lax.rem(tm + d, tm_count)
        return pltpu.make_async_remote_copy(
            src_ref=send.at[to],
            dst_ref=got.at[tm],
            send_sem=send_sems.at[d],
            recv_sem=recv_sems.at[d],
            device_id=(to, tb),
            device_id_type=MESH,
        )

    def backward(d):
        to = lax.rem(tm + d, tm_count)
        return pltpu.make_async_remote_copy(
            src_ref=entering.at[to],
            dst_ref=incoming.at[tm],
            send_sem=back_send_sems.at[d],
            recv_sem=back_recv_sems.at[d],
            device_id=(to, tb),
            device_id_type=MESH,
        )

    def sideways(d):
        to = lax.rem(tb + d, table_count)
        return pltpu.make_async_remote_copy(
            src_ref=ids_send.at[to],
            dst_ref=ids_got.at[tb],
            send_sem=ids_send_sems.at[d],
            recv_sem=ids_recv_sems.at[d],
            device_id=(tm, to),
            device_id_type=MESH,
        )

    def each(count, act):
        def body(d, carry):
            act(d)
            return carry

        lax.fori_loop(1, count, body, 0)

    each(tm_count, lambda d: outward(d).start())
    got[tm] = send[tm]

    lane = lax.broadcasted_iota(jnp.int32, (GROUP, LANES), 1)
    keep = lax.broadcasted_iota(jnp.int32, (GROUP, GROUP), 1) >= lax.broadcasted_iota(
        jnp.int32, (GROUP, GROUP), 0
    )

    def within(i, carry):
        b = blocks - 1 - i
        here = block_at(b, GROUP)
        rows = sums[block_at(b, HEADS), :]
        column = columns[here, :]
        scores = lax.dot_general(
            bc_ref[here, :STATE], bc_ref[here, STATE:], dims(1, 1), preferred_element_type=F32
        )
        for j in range(tiles):
            lanes = slice(j * LANES, (j + 1) * LANES)
            grad = grad_ref[here, lanes]
            total = None
            for k in range(per_tile):
                h = j * per_tile + k
                gaps = rows[h : h + 1, :] - column[:, h : h + 1]
                mixing = (jnp.exp(jnp.where(keep, gaps, -1e30)) * scores).astype(BF16)
                term = jnp.dot(mixing, grad, preferred_element_type=F32)
                term = term + skip_ref[h] * grad.astype(F32)
                total = term if total is None else jnp.where(lane >= k * head_dim, term, total)
            part[here, lanes] = total
        return carry

    first = blocks * 5 // 8
    lax.fori_loop(0, first, within, 0)

    each(tm_count, lambda d: outward(d).wait_recv())
    held = jnp.zeros((8, LANES), F32)
    for at in range(tm_count - 1, -1, -1):
        entering[at] = held
        held = got[at, 0] + got[at, 1] * held
    each(tm_count, lambda d: backward(d).start())
    incoming[tm] = entering[tm]
    for w in range(table_count):
        ids_send[w] = got[:, 2, w, :]
    each(table_count, lambda d: sideways(d).start())
    ids_got[tb] = ids_send[tb]

    lax.fori_loop(first, blocks, within, 0)

    each(tm_count, lambda d: backward(d).wait_recv())
    for r in range(STATE // 8):
        for j in range(tiles):
            state[8 * r : 8 * r + 8, j * LANES : (j + 1) * LANES] = incoming[r * tiles + j]

    def finish(i, carry):
        b = blocks - 1 - i
        here = block_at(b, GROUP)
        column = columns[here, :]
        fading = spread(jnp.exp(column[GROUP - 1 : GROUP, :] - column), width)
        carried = state[...]
        b_part = bc_ref[here, :STATE]
        product = jnp.dot(
            jnp.concatenate([b_part, b_part], axis=1),
            split(carried, 0),
            preferred_element_type=F32,
        )
        rows = (part[here, :] + product * fading).astype(BF16).astype(F32)
        fall = falls[block_at(b, 8), :]
        state[...] = ends[block_at(b, STATE), :] + fall[0:1, :] * carried
        for j in range(tiles):
            flat_ref[pl.ds(b * GROUP * tiles + j, GROUP, stride=tiles), :] = rows[
                :, j * LANES : (j + 1) * LANES
            ]
        return carry

    lax.fori_loop(0, blocks, finish, 0)
    each(table_count, lambda d: sideways(d).wait_recv())
    ids_ref[...] = ids_got[...]
    each(tm_count, lambda d: outward(d).wait_send())
    each(tm_count, lambda d: backward(d).wait_send())
    each(table_count, lambda d: sideways(d).wait_send())


def pack_kernel(place_ref, flat_ref, out_ref, packed):
    step = pl.program_id(0)
    tiles = out_ref.shape[1] // LANES

    @pl.when(step == 0)
    def _():
        packed[...] = jnp.zeros_like(packed)

    unroll = 16

    def place(s, carry):
        first = s * unroll
        to = [place_ref[step, first + i] for i in range(unroll)]
        rows = [
            flat_ref[pl.ds(pl.multiple_of((first + i) * tiles, tiles), tiles), :]
            for i in range(unroll)
        ]
        for i in range(unroll):
            packed[pl.ds(pl.multiple_of(to[i] * tiles, tiles), tiles), :] = rows[i]
        return carry

    lax.fori_loop(0, GROUP // unroll, place, 0)

    @pl.when(step == pl.num_programs(0) - 1)
    def _():
        chunk = 256

        def put(c, carry):
            for j in range(tiles):
                out_ref[
                    pl.ds(pl.multiple_of(c * chunk, chunk), chunk), j * LANES : (j + 1) * LANES
                ] = packed[pl.ds(c * chunk * tiles + j, chunk, stride=tiles), :].astype(BF16)
            return carry

        lax.fori_loop(0, out_ref.shape[0] // chunk, put, 0)


def update_kernel(ids_ref, rows_ref, table_ref, accum_ref, new_table_ref, new_accum_ref):
    tall = table_ref.shape[0]
    base = pl.program_id(0) * tall
    own = lax.broadcasted_iota(jnp.int32, (tall, ids_ref.shape[1]), 0) + base
    hits = jnp.where(own == ids_ref[...], 1.0, 0.0).astype(BF16)
    summed = jnp.dot(hits, rows_ref[...], preferred_element_type=F32)
    accum = accum_ref[...] + summed * summed
    new_accum_ref[...] = accum
    new_table_ref[...] = (
        table_ref[...].astype(F32) - RATE * summed / jnp.sqrt(accum)
    ).astype(BF16)


def on_device(out_grad, bc_proj, decay_log, skip_gain, owner, item_row, table, accum):
    users, events, width = out_grad.shape
    blocks = events // GROUP
    tiles = width // LANES
    tm_count = lax.axis_size("tm")
    table_count = lax.axis_size("table")
    holders = tm_count * table_count
    slots = holders * CAP
    vmem = pl.BlockSpec(memory_space=pltpu.VMEM)
    smem = pl.BlockSpec(memory_space=pltpu.SMEM)
    slices = (tm_count, 8, LANES)
    dma = pltpu.SemaphoreType.DMA

    flat, places, ids = pl.pallas_call(
        functools.partial(front_kernel, tm_count, table_count),
        name="front",
        out_shape=(
            jax.ShapeDtypeStruct((events * tiles, LANES), F32),
            jax.ShapeDtypeStruct((blocks, GROUP), jnp.int32),
            jax.ShapeDtypeStruct((table_count, tm_count, LANES), F32),
        ),
        in_specs=[vmem, vmem, vmem, vmem, vmem, smem],
        out_specs=(vmem, vmem, vmem),
        scratch_shapes=[
            pltpu.VMEM((events, HEADS), F32),
            pltpu.VMEM((blocks * HEADS, GROUP), F32),
            pltpu.VMEM((blocks * STATE, width), F32),
            pltpu.VMEM((blocks * 8, width), F32),
            pltpu.VMEM((events, width), F32),
            pltpu.VMEM((STATE, width), F32),
            pltpu.VMEM((8, width), F32),
            pltpu.VMEM((tm_count, 3, 8, LANES), F32),
            pltpu.VMEM((tm_count, 3, 8, LANES), F32),
            pltpu.VMEM(slices, F32),
            pltpu.VMEM(slices, F32),
            pltpu.VMEM((table_count, tm_count, LANES), F32),
            pltpu.VMEM((table_count, tm_count, LANES), F32),
            dma((tm_count,)),
            dma((tm_count,)),
            dma((tm_count,)),
            dma((tm_count,)),
            dma((table_count,)),
            dma((table_count,)),
        ],
        compiler_params=pltpu.CompilerParams(collective_id=0, has_side_effects=True),
    )(
        owner.reshape(1, events),
        item_row,
        out_grad.reshape(events, width),
        bc_proj.reshape(events, 2 * STATE),
        decay_log.reshape(HEADS, events),
        skip_gain,
    )
    got_ids = ids[:, :, :CAP].transpose(1, 0, 2).reshape(1, slots).astype(jnp.int32)

    send = pl.pallas_call(
        pack_kernel,
        name="pack",
        grid=(blocks,),
        out_shape=jax.ShapeDtypeStruct((slots, width), BF16),
        in_specs=[smem, pl.BlockSpec((GROUP * tiles, LANES), lambda i: (i, 0))],
        out_specs=pl.BlockSpec((slots, width), lambda i: (0, 0)),
        scratch_shapes=[pltpu.VMEM((slots * tiles, LANES), F32)],
    )(places, flat)

    got = lax.all_to_all(
        send.reshape(holders, CAP, width), ("tm", "table"), split_axis=0, concat_axis=0, tiled=True
    )

    owned = table.shape[0]
    tall = 256
    tile = pl.BlockSpec((tall, width), lambda i: (i, 0))
    return pl.pallas_call(
        update_kernel,
        name="update",
        grid=(owned // tall,),
        out_shape=(
            jax.ShapeDtypeStruct((owned, width), BF16),
            jax.ShapeDtypeStruct((owned, width), F32),
        ),
        in_specs=[
            pl.BlockSpec((1, slots), lambda i: (0, 0)),
            pl.BlockSpec((slots, width), lambda i: (0, 0)),
            tile,
            tile,
        ],
        out_specs=(tile, tile),
    )(got_ids, got.reshape(slots, width), table, accum)


def solution(mesh):
    placed = (
        P("table", "tm", None),
        P("table", "tm", None),
        P("table", None, "tm"),
        P(),
        P("table", "tm", None),
        P("table", "tm"),
        P(("tm", "table"), None),
        P(("tm", "table"), None),
    )
    return jax.shard_map(
        on_device,
        mesh=mesh,
        in_specs=placed,
        out_specs=(P(("tm", "table"), None), P(("tm", "table"), None)),
        check_vma=False,
    )
```
